32 devices in a mesh: seg: 4 (over y, x), sec: 8 (over z, core).
Axes of the slice: x: 2, y: 2, z: 4, core: 2. Of those that a mesh axis runs over, the one named last changes fastest.
Arguments:
- psi: float32 [4, 8, 256, 256], P('seg', 'sec'), may hold values from -17 to 17
- sector_dims: int32 [4, 8, 2], P('seg', 'sec'), may hold values from 64 to 256, as said below
- env_left: bfloat16 [4, 8, 30, 256, 256], P('seg', 'sec'), may hold values from -2 to 5
- env_right: bfloat16 [4, 8, 30, 256, 256], P('seg', 'sec'), may hold values from -2 to 5
Outputs:
- second_vector: float32 [4, 8, 256, 256], P('seg', 'sec')
- third_vector: float32 [4, 8, 256, 256], P('seg', 'sec')
- last_image: float32 [4, 8, 256, 256], P('seg', 'sec')
- coefficients: float32 [4, 5], P('seg')
- boundary: float32 [4, 8, 256, 256], P('seg', 'sec')
The draws below stay inside these ranges and needn't reach their ends.
Inputs may be any that keep to these rules, and one draw needn't show every extreme that they name: `sector_dims`: the largest live dimension of every segment is 256.
All inputs are finite; a program needn't handle non-finite values.
Results may differ from the reference program's by a relative error of at most 0.0095.
Values may be sent and summed in bfloat16 or wider, within the bound.
No kernel may reach another device: no remote copies, remote signals or barrier semaphores. Data moves between devices by JAX's collectives and lax.ppermute only.
A program may use at most 64 MiB of HBM per device.

```python
import jax
import jax.numpy as jnp
from jax import lax

SMAX = 256
W_ZERO = 6
W_HOP = 6
GRID = 4
TERMS = 30
NSEC = 8
SEGS = 4


def draw_psi(key, part):
    base_key = jax.random.fold_in(key, 0)
    sector = jnp.arange(NSEC, dtype=jnp.float32)
    values = jnp.clip(jax.random.normal(base_key, (SEGS, NSEC, SMAX, SMAX), jnp.float32), -5.0, 5.0)
    ramp = 1.0 + 2.0 * sector / (NSEC - 1)
    return values * ramp[None, :, None, None]


def draw_sector_dims(key, part):
    dims_key, pos_key = jax.random.split(key)
    dims = jax.random.randint(dims_key, (SEGS, NSEC, 2), SMAX // 4, SMAX + 1)
    where_full = jax.random.randint(pos_key, (SEGS, 1, 1), 0, NSEC)
    sector = jnp.arange(NSEC, dtype=jnp.int32)[None, :, None]
    return jnp.where(sector == where_full, SMAX, dims).astype(jnp.int32)


def environment(key):
    noise_key, diag_key = jax.random.split(key)
    shape = (SEGS, NSEC, TERMS, SMAX, SMAX)
    noise = jnp.clip(jax.random.normal(noise_key, shape, jnp.float32), -6.0, 6.0)
    diag_vals = jax.random.uniform(diag_key, (SEGS, NSEC, 1, SMAX, 1), jnp.float32, 1.0, 2.0)
    term_pos = lax.broadcasted_iota(jnp.int32, (1, 1, TERMS, 1, 1), 2)
    row_pos = lax.broadcasted_iota(jnp.int32, (1, 1, 1, SMAX, SMAX), 3)
    col_pos = lax.broadcasted_iota(jnp.int32, (1, 1, 1, SMAX, SMAX), 4)
    placed = ((term_pos == 1) & (row_pos == col_pos)).astype(jnp.float32)
    scaled = noise / jnp.sqrt(jnp.float32(SMAX)) + placed * diag_vals
    return scaled.astype(jnp.bfloat16)


def draw_env_left(key, part):
    return environment(jax.random.fold_in(key, 11))


def draw_env_right(key, part):
    return environment(jax.random.fold_in(key, 12))


def setup_inputs(seed: int = 0) -> dict:
    key_of = jax.random.split(jax.random.key(seed), 5)
    psi = draw_psi(jax.random.fold_in(key_of[4], 71), 0)
    sector_dims = draw_sector_dims(jax.random.fold_in(key_of[4], 71), 0)
    env_left = draw_env_left(jax.random.fold_in(key_of[4], 71), 0)
    env_right = draw_env_right(jax.random.fold_in(key_of[4], 71), 0)
    return {"psi": psi, "sector_dims": sector_dims, "env_left": env_left, "env_right": env_right}


EPSILON = 1e-06

def sector_mask(dims):
    idx = jnp.arange(SMAX, dtype=jnp.int32)
    left_live = (idx[None, :] < dims[:, 0:1]).astype(jnp.float32)
    right_live = (idx[None, :] < dims[:, 1:2]).astype(jnp.float32)
    return left_live[:, :, None] * right_live[:, None, :]

def neighbour_list(low):
    zero_one = jnp.zeros_like(low[:1])
    zero_grid = jnp.zeros_like(low[:GRID])
    sector = jnp.arange(NSEC, dtype=jnp.int32)
    column = sector % GRID
    row_pos = sector // GRID
    blocks = [jnp.concatenate([zero_one, low[:-1]]), jnp.concatenate([low[1:], zero_one]), jnp.concatenate([zero_grid, low[:-GRID]]), jnp.concatenate([low[GRID:], zero_grid])]
    flags = [column >= 1, column <= GRID - 2, row_pos >= 1, row_pos <= NSEC // GRID - 2]
    return [jnp.where(f[:, None, None], b, jnp.zeros_like(b)) for f, b in zip(flags, blocks)]

def contract(block, left_env, right_env, start, stop):
    inner = jnp.einsum('swij,sjk->swik', left_env[:, start:stop].astype(jnp.float32), block.astype(jnp.float32)).astype(jnp.bfloat16)
    return jnp.einsum('swik,swlk->sil', inner.astype(jnp.float32), right_env[:, start:stop].astype(jnp.float32))

def apply_operator(vector, left_env, right_env, mask):
    low = vector.astype(jnp.bfloat16)
    total = contract(low, left_env, right_env, 0, W_ZERO)
    for group, block in enumerate(neighbour_list(low)):
        start = W_ZERO + group * W_HOP
        total = total + contract(block, left_env, right_env, start, start + W_HOP)
    return total * mask

def one_segment(items):
    psi_seg, dims, left_env, right_env = items
    mask = sector_mask(dims)
    entries = jnp.float32(NSEC * SMAX * SMAX)
    start_vec = psi_seg * mask
    current = start_vec / jnp.sqrt(jnp.sum(start_vec * start_vec) / entries + EPSILON)
    image = apply_operator(current, left_env, right_env, mask)
    alpha0 = jnp.sum(image * current) / entries
    resid = image - alpha0 * current
    beta0 = jnp.sqrt(jnp.sum(resid * resid) / entries + EPSILON)
    second = resid / beta0
    image = apply_operator(second, left_env, right_env, mask)
    alpha1 = jnp.sum(image * second) / entries
    resid = image - alpha1 * second - beta0 * current
    beta1 = jnp.sqrt(jnp.sum(resid * resid) / entries + EPSILON)
    third = resid / beta1
    image = apply_operator(third, left_env, right_env, mask)
    alpha2 = jnp.sum(image * third) / entries
    return (second, third, image, jnp.stack([alpha0, alpha1, alpha2, beta0, beta1]))

def reference(psi, sector_dims, env_left, env_right):
    second, third, image, coeffs = lax.map(one_segment, (psi, sector_dims, env_left, env_right))
    own = third.astype(jnp.bfloat16)
    before = jnp.concatenate([jnp.zeros_like(own[:1]), own[:-1]])
    envpart = jnp.einsum('gsij,gsjk->gsik', env_left[:, :, 0].astype(jnp.float32), own.astype(jnp.float32)).astype(jnp.bfloat16)
    env_f = envpart.astype(jnp.float32)
    boundary = (jnp.einsum('gsji,gsjk->gsik', own.astype(jnp.float32), env_f) + jnp.einsum('gsji,gsjk->gsik', before.astype(jnp.float32), env_f)) / jnp.sqrt(jnp.float32(SMAX))
    return (second, third, image, coeffs, boundary)
```

```python
import functools

import jax
import jax.numpy as jnp
from jax import lax
from jax.experimental import pallas as pl
from jax.experimental.pallas import tpu as pltpu
from jax.sharding import PartitionSpec as P


W_ZERO = 6
W_HOP = 6
GRID = 4
EPSILON = 1e-06
SCALE = 2.0**-13
ROWS = 16

F32 = jnp.float32
BF16 = jnp.bfloat16


def matchings(count):
    found = {}
    for parity in (0, 1):
        pairs = []
        for s in range(count):
            c = s % GRID
            t = s + 1 if c % 2 == parity else s - 1
            if 0 <= c + (t - s) < GRID:
                pairs.append((s, t))
        if pairs:
            found[f"col{parity}"] = pairs
    for parity in (0, 1):
        pairs = []
        for s in range(count):
            r = s // GRID
            t = s + GRID if r % 2 == parity else s - GRID
            if 0 <= t < count:
                pairs.append((s, t))
        if pairs:
            found[f"row{parity}"] = pairs
    return found


def first_term(name):
    s = lax.axis_index("sec")
    place = lax.rem(s, GRID) if name[:3] == "col" else lax.div(s, GRID)
    ahead = lax.rem(place, 2) == int(name[3])
    base = W_ZERO if name[:3] == "col" else W_ZERO + 2 * W_HOP
    return jnp.where(ahead, base + W_HOP, base)


def contract(left, right, block):
    n, size = left.shape[0], left.shape[1]
    inner = jnp.dot(left.reshape(n * size, size), block, preferred_element_type=F32).astype(BF16)
    across = jnp.concatenate([inner[w * size : (w + 1) * size] for w in range(n)], axis=1)
    beside = jnp.concatenate([right[w] for w in range(n)], axis=1)
    return lax.dot_general(across, beside, (((1,), (1,)), ((), ())), preferred_element_type=F32)


def group(left_ref, right_ref, block, start, n):
    return contract(left_ref[0, 0, pl.ds(start, n)], right_ref[0, 0, pl.ds(start, n)], block)


def masked(value, dims_ref):
    rows = lax.broadcasted_iota(jnp.int32, value.shape, 0)
    cols = lax.broadcasted_iota(jnp.int32, value.shape, 1)
    keep = (rows < dims_ref[0, 0, 0]) & (cols < dims_ref[0, 0, 1])
    return jnp.where(keep, value, 0.0)


def row_sum(a, b):
    return jnp.sum(a * b, axis=0, keepdims=True)


def fold(v):
    out = v[:, :128]
    for k in range(1, v.shape[1] // 128):
        out = out + v[:, k * 128 : (k + 1) * 128]
    return out


def start_kernel(psi_ref, dims_ref, x_ref, low_ref):
    x = masked(psi_ref[0, 0], dims_ref)
    x_ref[...] = x
    low_ref[...] = x.astype(BF16)


def early_kernel(names, left_ref, right_ref, low_ref, *refs):
    blocks, out_ref = refs[:-1], refs[-1]
    total = group(left_ref, right_ref, low_ref[...], 0, W_ZERO)
    for name, ref in zip(names, blocks):
        total = total + group(left_ref, right_ref, ref[...], first_term(name), W_HOP)
    out_ref[...] = total


def late_kernel(names, left_ref, right_ref, dims_ref, total_ref, *refs):
    blocks, u_ref, low_ref = refs[: len(names)], refs[-2], refs[-1]
    total = total_ref[...]
    for name, ref in zip(names, blocks):
        total = total + group(left_ref, right_ref, ref[...], first_term(name), W_HOP)
    u = masked(total * SCALE, dims_ref)
    u_ref[...] = u
    low_ref[...] = u.astype(BF16)


def dots_kernel(u0_ref, u1_ref, u2_ref, u3_ref, out_ref):
    u = [r[...] for r in (u0_ref, u1_ref, u2_ref, u3_ref)]
    out_ref[...] = jnp.zeros_like(out_ref)
    for place, (i, j) in enumerate(PAIRS):
        out_ref[place : place + 1] = fold(row_sum(u[i], u[j]))


PAIRS = [(0, 0), (0, 1), (1, 1), (0, 2), (1, 2), (2, 2), (0, 3), (1, 3), (2, 3)]


def solve(sums, entries):
    table = {}
    for place, (i, j) in enumerate(PAIRS):
        table[i, j] = table[j, i] = jnp.sum(sums[place : place + 1], axis=(0, 1), keepdims=True)
    zero = jnp.zeros((1, 1), F32)

    def dot(c, d):
        out = zero
        for i, a in enumerate(c):
            for j, b in enumerate(d):
                if a is not None and b is not None:
                    out = out + a * b * table[i, j]
        return out

    def apply(c):
        return [None] + [None if a is None else a * (1.0 / SCALE) for a in c]

    inv = 1.0 / entries
    v0 = [1.0 / jnp.sqrt(table[0, 0] * inv + EPSILON)]
    w = apply(v0)
    alpha0 = dot(w, v0) * inv
    r = [-alpha0 * v0[0], w[1]]
    beta0 = jnp.sqrt(dot(r, r) * inv + EPSILON)
    second = [c / beta0 for c in r]
    w = apply(second)
    alpha1 = dot(w, second) * inv
    r = [-alpha1 * second[0] - beta0 * v0[0], w[1] - alpha1 * second[1], w[2]]
    beta1 = jnp.sqrt(dot(r, r) * inv + EPSILON)
    third = [c / beta1 for c in r]
    image = apply(third)
    alpha2 = dot(image, third) * inv
    return second, third, image, [alpha0, alpha1, alpha2, beta0, beta1]


def combine(coefs, refs):
    out = None
    for c, r in zip(coefs, refs):
        if c is not None:
            out = c * r[...] if out is None else out + c * r[...]
    return out


def third_kernel(entries, sums_ref, u0_ref, u1_ref, u2_ref, third_ref, own_ref):
    _, coefs, _, _ = solve(sums_ref[...], entries)
    third = combine(coefs, (u0_ref, u1_ref, u2_ref))
    third_ref[0, 0] = third
    own_ref[...] = third.astype(BF16)


def rest_kernel(
    entries, sums_ref, u0_ref, u1_ref, u2_ref, u3_ref, left_ref, own_ref,
    second_ref, image_ref, coef_ref, env_ref,
):
    second, _, image, values = solve(sums_ref[...], entries)
    us = (u0_ref, u1_ref, u2_ref, u3_ref)
    second_ref[0, 0] = combine(second, us)
    image_ref[0, 0] = combine(image, us)
    for place, value in enumerate(values):
        coef_ref[:, place : place + 1] = value
    env_ref[...] = jnp.dot(
        left_ref[0, 0, 0], own_ref[...], preferred_element_type=F32
    ).astype(BF16)


def boundary_kernel(own_ref, before_ref, env_ref, out_ref):
    dims = (((0,), (0,)), ((), ()))
    total = lax.dot_general(own_ref[...], env_ref[...], dims, preferred_element_type=F32)
    total = total + lax.dot_general(
        before_ref[...], env_ref[...], dims, preferred_element_type=F32
    )
    out_ref[0, 0] = total * (1.0 / total.shape[0] ** 0.5)


def kernel_call(body, out_shape, spaces, flops):
    def spec(space):
        return pl.BlockSpec(memory_space=space)

    return pl.pallas_call(
        body,
        out_shape=out_shape,
        in_specs=[spec(pltpu.SMEM if s == "s" else pltpu.VMEM) for s in spaces],
        out_specs=jax.tree.map(lambda _: spec(pltpu.VMEM), out_shape),
        compiler_params=pltpu.CompilerParams(vmem_limit_bytes=24 << 20),
        cost_estimate=pl.CostEstimate(flops=flops, bytes_accessed=0, transcendentals=0),
    )


def body(psi, sector_dims, env_left, env_right):
    size = psi.shape[-1]
    count = lax.axis_size("sec")
    entries = float(count * size * size)
    block32 = jax.ShapeDtypeStruct((size, size), F32)
    block16 = jax.ShapeDtypeStruct((size, size), BF16)
    swaps = matchings(count)
    early = [n for n in swaps if n == "col0"]
    late = [n for n in swaps if n[:3] == "row"] + [n for n in swaps if n == "col1"]
    sent = [n for n in swaps if n[:3] == "row"] + [n for n in swaps if n[:3] == "col"]
    product = 2 * 2 * size**3

    x, low = kernel_call(start_kernel, (block32, block16), "vs", 0)(psi, sector_dims)
    vectors = [x]
    for _ in range(3):
        found = {}
        for n in sent:
            found[n] = lax.ppermute(low, "sec", swaps[n])
        total = kernel_call(
            functools.partial(early_kernel, early),
            block32,
            "vvv" + "v" * len(early),
            product * (W_ZERO + W_HOP * len(early)),
        )(env_left, env_right, low, *[found[n] for n in early])
        u, low = kernel_call(
            functools.partial(late_kernel, late),
            (block32, block16),
            "vvsv" + "v" * len(late),
            product * W_HOP * len(late),
        )(env_left, env_right, sector_dims, total, *[found[n] for n in late])
        vectors.append(u)
    sums = kernel_call(dots_kernel, jax.ShapeDtypeStruct((ROWS, 128), F32), "vvvv", 0)(*vectors)
    hop = 1
    while hop < count:
        sums = sums + lax.ppermute(sums, "sec", [(i, i ^ hop) for i in range(count)])
        hop *= 2
    full = jax.ShapeDtypeStruct((1, 1, size, size), F32)
    third, own = kernel_call(
        functools.partial(third_kernel, entries), (full, block16), "vvvv", 0
    )(sums, *vectors[:3])
    segs = lax.axis_size("seg")
    before = lax.ppermute(own, "seg", [(g, g + 1) for g in range(segs - 1)])
    second, image, coefs, env = kernel_call(
        functools.partial(rest_kernel, entries),
        (full, full, jax.ShapeDtypeStruct((1, 5), F32), block16),
        "vvvvvvv",
        2 * size**3,
    )(sums, *vectors, env_left, own)
    boundary = kernel_call(boundary_kernel, full, "vvv", 4 * size**3)(
        own, before, env
    )
    return second, third, image, coefs, boundary


def solution(mesh):
    count = mesh.shape["sec"]
    assert count & (count - 1) == 0
    in_specs = (
        P("seg", "sec", None, None),
        P("seg", "sec", None),
        P("seg", "sec", None, None, None),
        P("seg", "sec", None, None, None),
    )
    out_specs = (
        P("seg", "sec", None, None),
        P("seg", "sec", None, None),
        P("seg", "sec", None, None),
        P("seg", None),
        P("seg", "sec", None, None),
    )
    return jax.shard_map(body, mesh=mesh, in_specs=in_specs, out_specs=out_specs, check_vma=False)
```

```python
import functools

import jax
import jax.numpy as jnp
from jax import lax
from jax.experimental import pallas as pl
from jax.experimental.pallas import tpu as pltpu
from jax.sharding import PartitionSpec as P


W_ZERO = 6
W_HOP = 6
GRID = 4
EPSILON = 1e-06
SCALE = 2.0**-13
LOW_PAIRS = ((0, 0), (0, 1), (1, 1), (0, 2), (1, 2), (2, 2))
TOP_PAIRS = ((0, 3), (1, 3), (2, 3))

F32 = jnp.float32
BF16 = jnp.bfloat16


def routes(count):
    rows = count // GRID
    assert rows % 2 == 0 and GRID == 4
    first, across, second, between = {}, {}, {}, {}
    for s in range(count):
        r, c = divmod(s, GRID)
        over = s + GRID if r % 2 == 0 else s - GRID
        side = s + 1 if c == 1 else s - 1
        across[s] = s + 1 if c % 2 == 0 else s - 1
        if c in (0, GRID - 1):
            first[s] = over
        else:
            first[s], second[s] = side, over
        beyond = s - GRID if r % 2 == 0 else s + GRID
        if 0 <= beyond < count:
            between[s] = beyond
    found = {"first": first, "across": across, "second": second}
    if between:
        found["between"] = between
    return found


def permute(block, route):
    segs, count = lax.axis_size("seg"), lax.axis_size("sec")
    pairs = []
    for g in range(segs):
        for target in range(count):
            if target in route:
                pairs.append((g * count + route[target], g * count + target))
            else:
                pairs.append(((g ^ 1) * count + target, g * count + target))
    return lax.ppermute(block, ("seg", "sec"), pairs)


def reached(route):
    s = lax.axis_index("sec")
    return functools.reduce(jnp.logical_or, [s == t for t in route])


def first_term(route):
    place = {-1: 0, 1: 1, -GRID: 2, GRID: 3}
    s = lax.axis_index("sec")
    start = jnp.int32(0)
    for target, source in route.items():
        start = jnp.where(s == target, W_ZERO + W_HOP * place[source - target], start)
    return start


def split(value):
    high = value.astype(BF16)
    return high, (value - high.astype(F32)).astype(BF16)


def beside(parts):
    return jnp.concatenate(parts, axis=1)


def contract(left, right, block, rest=None, fine=False):
    n, size = left.shape[0], left.shape[1]
    tall = left.reshape(n * size, size)
    inner = jnp.dot(tall, block, preferred_element_type=F32)
    if rest is not None:
        inner = inner + jnp.dot(tall, rest, preferred_element_type=F32)
    pieces = split(inner) if fine else (inner.astype(BF16),)
    a = beside([p[w * size : (w + 1) * size] for p in pieces for w in range(n)])
    b = beside([right[w] for w in range(n)] * len(pieces))
    return lax.dot_general(a, b, (((1,), (1,)), ((), ())), preferred_element_type=F32)


def slot(ref, k):
    return ref[k * W_HOP : (k + 1) * W_HOP]


def row_dot(a, b):
    total = jnp.sum(a * b, axis=0, keepdims=True)
    return sum(total[:, k : k + 128] for k in range(0, total.shape[1], 128))


def start_kernel(psi_hbm, dims_hbm, x_ref, low_ref, mask_ref, psi_ref, dims_ref, sems):
    copies = (
        pltpu.make_async_copy(dims_hbm.at[0], dims_ref, sems.at[0]),
        pltpu.make_async_copy(psi_hbm.at[0, 0], psi_ref, sems.at[1]),
    )
    for c in copies:
        c.start()
    for c in copies:
        c.wait()
    rows = lax.broadcasted_iota(jnp.int32, mask_ref.shape, 0)
    cols = lax.broadcasted_iota(jnp.int32, mask_ref.shape, 1)
    keep = (rows < dims_ref[0, 0]) & (cols < dims_ref[0, 1])
    x = jnp.where(keep, psi_ref[...], 0.0)
    x_ref[...] = x
    low_ref[...] = x.astype(BF16)
    mask_ref[...] = jnp.where(keep, SCALE, 0.0)


def load_kernel(
    ways, left_hbm, right_hbm, low_ref, across_ref, total_ref, left_ref, right_ref, sems
):
    starts = [0] + [first_term(w) for w in ways]
    copies = []
    for k, start in enumerate(starts):
        for side, (hbm, ref) in enumerate(((left_hbm, left_ref), (right_hbm, right_ref))):
            copies.append(
                pltpu.make_async_copy(
                    hbm.at[0, 0, pl.ds(start, W_HOP)],
                    ref.at[pl.ds(k * W_HOP, W_HOP)],
                    sems.at[2 * k + side],
                )
            )
    for c in copies:
        c.start()
    for c in copies[:2]:
        c.wait()
    total = contract(slot(left_ref, 0), slot(right_ref, 0), low_ref[...])
    for c in copies[2:4]:
        c.wait()
    total_ref[...] = total + contract(slot(left_ref, 1), slot(right_ref, 1), across_ref[...])
    for c in copies[4:]:
        c.wait()


def early_kernel(left_ref, right_ref, low_ref, across_ref, out_ref):
    out_ref[...] = contract(slot(left_ref, 0), slot(right_ref, 0), low_ref[...]) + contract(
        slot(left_ref, 1), slot(right_ref, 1), across_ref[...]
    )


def middle_kernel(left_ref, right_ref, total_ref, block_ref, out_ref):
    out_ref[...] = total_ref[...] + contract(
        slot(left_ref, 2), slot(right_ref, 2), block_ref[...]
    )


def image_into(u_ref, ways, left_ref, right_ref, mask_ref, total_ref, blocks):
    u_ref[...] = total_ref[...]
    for k, (way, ref) in enumerate(zip(ways, blocks)):

        @pl.when(reached(way))
        def _():
            u_ref[...] += contract(slot(left_ref, 3 + k), slot(right_ref, 3 + k), ref[...])

    u = u_ref[...] * mask_ref[...]
    u_ref[...] = u
    return u


def late_kernel(ways, packed, left_ref, right_ref, mask_ref, total_ref, *refs):
    n = len(ways)
    if packed:
        before_ref, u_ref, low_ref, pack_ref = refs[n:]
    else:
        u_ref, low_ref = refs[n:]
    u = image_into(u_ref, ways, left_ref, right_ref, mask_ref, total_ref, refs[:n])
    low = u.astype(BF16)
    low_ref[...] = low
    if packed:
        size = u.shape[0]
        pack_ref[:size] = before_ref[...]
        pack_ref[size:] = low


def last_kernel(ways, left_ref, right_ref, mask_ref, total_ref, *refs):
    n = len(ways)
    u0_ref, u1_ref, u2_ref, u_ref, dots_ref = refs[n:]
    u = image_into(u_ref, ways, left_ref, right_ref, mask_ref, total_ref, refs[:n])
    dots_ref[...] = jnp.zeros_like(dots_ref)
    for place, ref in enumerate((u0_ref, u1_ref, u2_ref)):
        dots_ref[place : place + 1] = row_dot(ref[...], u)


def gram_kernel(u0_ref, u1_ref, u2_ref, dots_ref):
    u = [r[...] for r in (u0_ref, u1_ref, u2_ref)]
    dots_ref[...] = jnp.zeros_like(dots_ref)
    for place, (i, j) in enumerate(LOW_PAIRS):
        dots_ref[place : place + 1] = row_dot(u[i], u[j])


def join_kernel(low_ref, top_ref, prior_ref, out_ref):
    out_ref[:8] = low_ref[...]
    out_ref[8:16] = top_ref[...]
    out_ref[16:] = prior_ref[...]


def table_of(sums, low, top=None):
    table = {}
    for first, pairs in ((low, LOW_PAIRS), (top, TOP_PAIRS)):
        if first is not None:
            for place, (i, j) in enumerate(pairs):
                row = sums[first + place : first + place + 1]
                table[i, j] = table[j, i] = jnp.sum(row, axis=(0, 1), keepdims=True)
    return table


def apply(c):
    return [None] + [None if a is None else a * (1.0 / SCALE) for a in c]


def solve(table, entries):
    def dot(c, d):
        out = jnp.zeros((1, 1), F32)
        for i, a in enumerate(c):
            for j, b in enumerate(d):
                if a is not None and b is not None:
                    out = out + a * b * table[i, j]
        return out

    inv = 1.0 / entries
    v0 = [1.0 / jnp.sqrt(table[0, 0] * inv + EPSILON)]
    w = apply(v0)
    alpha0 = dot(w, v0) * inv
    r = [-alpha0 * v0[0], w[1]]
    beta0 = jnp.sqrt(dot(r, r) * inv + EPSILON)
    second = [c / beta0 for c in r]
    w = apply(second)
    alpha1 = dot(w, second) * inv
    r = [-alpha1 * second[0] - beta0 * v0[0], w[1] - alpha1 * second[1], w[2]]
    beta1 = jnp.sqrt(dot(r, r) * inv + EPSILON)
    third = [c / beta1 for c in r]
    values = [alpha0, alpha1, None, beta0, beta1]
    image = apply(third)
    if (0, 3) in table:
        values[2] = dot(image, third) * inv
    return second, third, image, values


def combine(coefs, blocks):
    out = None
    for c, b in zip(coefs, blocks):
        if c is not None:
            out = c * b if out is None else out + c * b
    return out


def end_kernel(
    entries, sums_ref, u0_ref, u1_ref, u2_ref, u3_ref, left_ref, prev01_ref, prev2_ref,
    second_ref, third_ref, image_ref, coef_ref, boundary_ref,
):
    sums = sums_ref[...]
    second, third, image, values = solve(table_of(sums, 0, 8), entries)
    _, prior, _, _ = solve(table_of(sums, 16), entries)
    us = [r[...] for r in (u0_ref, u1_ref, u2_ref, u3_ref)]
    size = us[0].shape[0]
    vector = combine(third, us)
    own = vector.astype(BF16)
    lows = (prev01_ref[:size], prev01_ref[size:], prev2_ref[...])
    before = combine(prior, [v.astype(F32) for v in lows])
    before = jnp.where(lax.axis_index("seg") > 0, before, 0.0).astype(BF16)
    env = jnp.dot(left_ref[0], own, preferred_element_type=F32).astype(BF16)
    dims = (((0,), (0,)), ((), ()))
    total = lax.dot_general(own, env, dims, preferred_element_type=F32)
    total = total + lax.dot_general(before, env, dims, preferred_element_type=F32)
    boundary_ref[0, 0] = total * (1.0 / size**0.5)
    third_ref[0, 0] = vector
    second_ref[0, 0] = combine(second, us)
    image_ref[0, 0] = combine(image, us)
    for place, value in enumerate(values):
        coef_ref[:, place : place + 1] = value


def kernel_call(body, out_shape, n_in, hbm=(), scratch=(), flops=0, moved=0):
    def spec(k):
        return pl.BlockSpec(memory_space=pl.ANY if k in hbm else pltpu.VMEM)

    return pl.pallas_call(
        body,
        out_shape=out_shape,
        in_specs=[spec(k) for k in range(n_in)],
        out_specs=jax.tree.map(lambda _: pl.BlockSpec(memory_space=pltpu.VMEM), out_shape),
        scratch_shapes=scratch,
        compiler_params=pltpu.CompilerParams(vmem_limit_bytes=24 << 20),
        cost_estimate=pl.CostEstimate(flops=flops, bytes_accessed=moved, transcendentals=0),
    )


def body(psi, sector_dims, env_left, env_right):
    size = psi.shape[-1]
    count, segs = lax.axis_size("sec"), lax.axis_size("seg")
    entries = float(count * size * size)

    def block(dtype, rows=size):
        return jax.ShapeDtypeStruct((rows, size), dtype)

    eight = jax.ShapeDtypeStruct((8, 128), F32)
    ways = routes(count)
    late = list(ways)[2:]
    last_ways = [ways[n] for n in late]
    onward = [(g, (g + 1) % segs) for g in range(segs)]
    product = 2 * 2 * size**3 * W_HOP

    def in_hbm(a):
        return pltpu.with_memory_space_constraint(a, pltpu.HBM)

    x, low, mask = kernel_call(
        start_kernel,
        (block(F32), block(BF16), block(F32)),
        2,
        hbm=(0, 1),
        scratch=[
            pltpu.VMEM((size, size), F32),
            pltpu.SMEM((1, 2), jnp.int32),
            pltpu.SemaphoreType.DMA((2,)),
        ],
        moved=2**20,
    )(in_hbm(psi), in_hbm(sector_dims))
    us = [x]
    for step in range(3):
        found = {}
        for n, way in ways.items():
            found[n] = permute(low, way)
        if step == 1:
            prev01 = lax.ppermute(pack, "seg", onward)
        if step == 2:
            dots = kernel_call(gram_kernel, eight, 3)(*us)
            prior = lax.ppermute(dots, "seg", onward)
            prev2 = lax.ppermute(low, "seg", onward)
        if step == 0:
            slots = 1 + len(ways)
            held = pltpu.VMEM((slots * W_HOP, size, size), BF16)
            total, left, right = kernel_call(
                functools.partial(load_kernel, [ways["across"], ways["first"]] + [ways[n] for n in late]),
                (block(F32), held, held),
                4,
                hbm=(0, 1),
                scratch=[pltpu.SemaphoreType.DMA((2 * slots,))],
                flops=2 * product,
                moved=8 << 20,
            )(in_hbm(env_left), in_hbm(env_right), low, found["across"])
        else:
            total = kernel_call(early_kernel, block(F32), 4, flops=2 * product)(
                left, right, low, found["across"]
            )
        total = kernel_call(middle_kernel, block(F32), 4, flops=product)(
            left, right, total, found["first"]
        )
        args = (left, right, mask, total, *[found[n] for n in late])
        n = len(late)
        if step == 0:
            u, low, pack = kernel_call(
                functools.partial(late_kernel, last_ways, True),
                (block(F32), block(BF16), block(BF16, 2 * size)),
                5 + n,
                flops=n * product,
            )(*args, low)
        elif step == 1:
            u, low = kernel_call(
                functools.partial(late_kernel, last_ways, False),
                (block(F32), block(BF16)),
                4 + n,
                flops=n * product,
            )(*args)
        else:
            u, top = kernel_call(
                functools.partial(last_kernel, last_ways),
                (block(F32), eight),
                7 + n,
                flops=n * product,
            )(*args, *us)
        us.append(u)
    sums = kernel_call(join_kernel, jax.ShapeDtypeStruct((24, 128), F32), 3)(dots, top, prior)
    hop = 1
    while hop < count:
        sums = sums + lax.ppermute(sums, "sec", [(i, i ^ hop) for i in range(count)])
        hop *= 2
    full = jax.ShapeDtypeStruct((1, 1, size, size), F32)
    return tuple(
        kernel_call(
            functools.partial(end_kernel, entries),
            (full, full, full, jax.ShapeDtypeStruct((1, 5), F32), full),
            8,
            flops=6 * size**3,
        )(sums, *us, left, prev01, prev2)
    )


def solution(mesh):
    count = mesh.shape["sec"]
    assert count & (count - 1) == 0
    in_specs = (
        P("seg", "sec", None, None),
        P("seg", "sec", None),
        P("seg", "sec", None, None, None),
        P("seg", "sec", None, None, None),
    )
    out_specs = (
        P("seg", "sec", None, None),
        P("seg", "sec", None, None),
        P("seg", "sec", None, None),
        P("seg", None),
        P("seg", "sec", None, None),
    )
    return jax.shard_map(body, mesh=mesh, in_specs=in_specs, out_specs=out_specs, check_vma=False)
```

```python
import functools

import jax
import jax.numpy as jnp
from jax import lax
from jax.experimental import pallas as pl
from jax.experimental.pallas import tpu as pltpu
from jax.sharding import PartitionSpec as P


W_ZERO = 6
W_HOP = 6
GRID = 4
EPSILON = 1e-06
PARTS = 2
SCALE = 2.0**-13
LOW_PAIRS = ((0, 0), (0, 1), (1, 1), (0, 2), (1, 2), (2, 2))
TOP_PAIRS = ((0, 3), (1, 3), (2, 3))

F32 = jnp.float32
BF16 = jnp.bfloat16


def routes(count):
    rows = count // GRID
    assert rows % 2 == 0 and GRID == 4
    first, across, second, between = {}, {}, {}, {}
    for s in range(count):
        r, c = divmod(s, GRID)
        over = s + GRID if r % 2 == 0 else s - GRID
        side = s + 1 if c == 1 else s - 1
        across[s] = s + 1 if c % 2 == 0 else s - 1
        if c in (0, GRID - 1):
            first[s] = over
        else:
            first[s], second[s] = side, over
        beyond = s - GRID if r % 2 == 0 else s + GRID
        if 0 <= beyond < count:
            between[s] = beyond
    found = {"first": first, "across": across, "second": second}
    if between:
        found["between"] = between
    return found


def permute(block, route):
    segs, count = lax.axis_size("seg"), lax.axis_size("sec")
    pairs = []
    for g in range(segs):
        for target in range(count):
            if target in route:
                pairs.append((g * count + route[target], g * count + target))
            else:
                pairs.append(((g ^ 1) * count + target, g * count + target))
    return lax.ppermute(block, ("seg", "sec"), pairs)


def reached(route):
    s = lax.axis_index("sec")
    return functools.reduce(jnp.logical_or, [s == t for t in route])


def first_term(route):
    place = {-1: 0, 1: 1, -GRID: 2, GRID: 3}
    s = lax.axis_index("sec")
    start = jnp.int32(0)
    for target, source in route.items():
        start = jnp.where(s == target, W_ZERO + W_HOP * place[source - target], start)
    return start


def split(value):
    high = value.astype(BF16)
    return high, (value - high.astype(F32)).astype(BF16)


def beside(parts):
    return jnp.concatenate(parts, axis=1)


def contract(left, right, block, rest=None, fine=False):
    n, size = left.shape[0], left.shape[1]
    tall = left.reshape(n * size, size)
    inner = jnp.dot(tall, block, preferred_element_type=F32)
    if rest is not None:
        inner = inner + jnp.dot(tall, rest, preferred_element_type=F32)
    pieces = split(inner) if fine else (inner.astype(BF16),)
    a = beside([p[w * size : (w + 1) * size] for p in pieces for w in range(n)])
    b = beside([right[w] for w in range(n)] * len(pieces))
    return lax.dot_general(a, b, (((1,), (1,)), ((), ())), preferred_element_type=F32)


def slot(ref, k):
    return ref[k * W_HOP : (k + 1) * W_HOP]


def row_dot(a, b):
    total = jnp.sum(a * b, axis=0, keepdims=True)
    return sum(total[:, k : k + 128] for k in range(0, total.shape[1], 128))


def start_kernel(psi_hbm, dims_hbm, x_ref, low_ref, mask_ref, psi_ref, dims_ref, sems):
    tall = psi_ref.shape[0] // PARTS
    copies = [pltpu.make_async_copy(dims_hbm.at[0], dims_ref, sems.at[0])]
    for k in range(PARTS):
        part = pl.ds(k * tall, tall)
        copies.append(
            pltpu.make_async_copy(psi_hbm.at[0, 0, part], psi_ref.at[part], sems.at[1 + k])
        )
    for c in copies:
        c.start()
    copies[0].wait()
    cols = lax.broadcasted_iota(jnp.int32, (tall, psi_ref.shape[1]), 1)
    live = cols < dims_ref[0, 1]
    for k in range(PARTS):
        part = pl.ds(k * tall, tall)
        rows = k * tall + lax.broadcasted_iota(jnp.int32, live.shape, 0)
        keep = live & (rows < dims_ref[0, 0])
        mask_ref[part] = jnp.where(keep, SCALE, 0.0)
        copies[1 + k].wait()
        x = jnp.where(keep, psi_ref[part], 0.0)
        x_ref[part] = x
        low_ref[part] = x.astype(BF16)


def load_kernel(
    ways, left_hbm, right_hbm, low_ref, across_ref, total_ref, left_ref, right_ref, sems
):
    starts = [0] + [first_term(w) for w in ways]
    copies = []
    for k, start in enumerate(starts):
        for side, (hbm, ref) in enumerate(((left_hbm, left_ref), (right_hbm, right_ref))):
            copies.append(
                pltpu.make_async_copy(
                    hbm.at[0, 0, pl.ds(start, W_HOP)],
                    ref.at[pl.ds(k * W_HOP, W_HOP)],
                    sems.at[2 * k + side],
                )
            )
    for c in copies:
        c.start()
    for c in copies[:2]:
        c.wait()
    total = contract(slot(left_ref, 0), slot(right_ref, 0), low_ref[...])
    for c in copies[2:4]:
        c.wait()
    total_ref[...] = total + contract(slot(left_ref, 1), slot(right_ref, 1), across_ref[...])
    for c in copies[4:]:
        c.wait()


def early_kernel(left_ref, right_ref, low_ref, across_ref, out_ref):
    out_ref[...] = contract(slot(left_ref, 0), slot(right_ref, 0), low_ref[...]) + contract(
        slot(left_ref, 1), slot(right_ref, 1), across_ref[...]
    )


def middle_kernel(left_ref, right_ref, total_ref, block_ref, out_ref):
    out_ref[...] = total_ref[...] + contract(
        slot(left_ref, 2), slot(right_ref, 2), block_ref[...]
    )


def image_into(u_ref, low_ref, ways, left_ref, right_ref, mask_ref, total_ref, blocks):
    def part(k):
        return contract(slot(left_ref, 3 + k), slot(right_ref, 3 + k), blocks[k][...])

    def finish(total):
        u = total * mask_ref[...]
        u_ref[...] = u
        if low_ref is not None:
            low_ref[...] = u.astype(BF16)

    so_far = total_ref
    for k, way in enumerate(ways[:-1]):
        if k == 0:
            u_ref[...] = total_ref[...]
            so_far = u_ref

        @pl.when(reached(way))
        def _():
            u_ref[...] += part(k)

    here = reached(ways[-1])

    @pl.when(here)
    def _():
        finish(so_far[...] + part(len(ways) - 1))

    @pl.when(jnp.logical_not(here))
    def _():
        finish(so_far[...])


def late_kernel(ways, packed, left_ref, right_ref, mask_ref, total_ref, *refs):
    n = len(ways)
    if packed:
        before_ref, u_ref, low_ref, pack_ref = refs[n:]
    else:
        u_ref, low_ref = refs[n:]
    image_into(u_ref, low_ref, ways, left_ref, right_ref, mask_ref, total_ref, refs[:n])
    if packed:
        size = low_ref.shape[0]
        pack_ref[:size] = before_ref[...]
        pack_ref[size:] = low_ref[...]


def last_kernel(ways, left_ref, right_ref, mask_ref, total_ref, *refs):
    n = len(ways)
    u0_ref, u1_ref, u2_ref, u_ref, dots_ref = refs[n:]
    image_into(u_ref, None, ways, left_ref, right_ref, mask_ref, total_ref, refs[:n])
    u = u_ref[...]
    dots_ref[...] = jnp.zeros_like(dots_ref)
    for place, ref in enumerate((u0_ref, u1_ref, u2_ref)):
        dots_ref[place : place + 1] = row_dot(ref[...], u)


def gram_kernel(u0_ref, u1_ref, u2_ref, dots_ref):
    u = [r[...] for r in (u0_ref, u1_ref, u2_ref)]
    dots_ref[...] = jnp.zeros_like(dots_ref)
    for place, (i, j) in enumerate(LOW_PAIRS):
        dots_ref[place : place + 1] = row_dot(u[i], u[j])


def join_kernel(low_ref, top_ref, prior_ref, out_ref):
    out_ref[:8] = low_ref[...]
    out_ref[8:16] = top_ref[...]
    out_ref[16:] = prior_ref[...]


def table_of(sums, low, top=None):
    table = {}
    for first, pairs in ((low, LOW_PAIRS), (top, TOP_PAIRS)):
        if first is not None:
            for place, (i, j) in enumerate(pairs):
                row = sums[first + place : first + place + 1]
                table[i, j] = table[j, i] = jnp.sum(row, axis=(0, 1), keepdims=True)
    return table


def apply(c):
    return [None] + [None if a is None else a * (1.0 / SCALE) for a in c]


def solve(table, entries):
    def dot(c, d):
        out = jnp.zeros((1, 1), F32)
        for i, a in enumerate(c):
            for j, b in enumerate(d):
                if a is not None and b is not None:
                    out = out + a * b * table[i, j]
        return out

    inv = 1.0 / entries
    v0 = [1.0 / jnp.sqrt(table[0, 0] * inv + EPSILON)]
    w = apply(v0)
    alpha0 = dot(w, v0) * inv
    r = [-alpha0 * v0[0], w[1]]
    beta0 = jnp.sqrt(dot(r, r) * inv + EPSILON)
    second = [c / beta0 for c in r]
    w = apply(second)
    alpha1 = dot(w, second) * inv
    r = [-alpha1 * second[0] - beta0 * v0[0], w[1] - alpha1 * second[1], w[2]]
    beta1 = jnp.sqrt(dot(r, r) * inv + EPSILON)
    third = [c / beta1 for c in r]
    values = [alpha0, alpha1, None, beta0, beta1]
    image = apply(third)
    if (0, 3) in table:
        values[2] = dot(image, third) * inv
    return second, third, image, values


def combine(coefs, blocks):
    out = None
    for c, b in zip(coefs, blocks):
        if c is not None:
            out = c * b if out is None else out + c * b
    return out


def end_kernel(
    entries, sums_ref, u0_ref, u1_ref, u2_ref, u3_ref, left_ref, prev01_ref, prev2_ref,
    second_ref, third_ref, image_ref, coef_ref, boundary_ref,
):
    sums = sums_ref[...]
    second, third, image, values = solve(table_of(sums, 0, 8), entries)
    _, prior, _, _ = solve(table_of(sums, 16), entries)
    us = [r[...] for r in (u0_ref, u1_ref, u2_ref, u3_ref)]
    size = us[0].shape[0]
    vector = combine(third, us)
    own = vector.astype(BF16)
    lows = (prev01_ref[:size], prev01_ref[size:], prev2_ref[...])
    before = combine(prior, [v.astype(F32) for v in lows])
    before = jnp.where(lax.axis_index("seg") > 0, before, 0.0).astype(BF16)
    env = jnp.dot(left_ref[0], own, preferred_element_type=F32).astype(BF16)
    dims = (((0,), (0,)), ((), ()))
    total = lax.dot_general(own, env, dims, preferred_element_type=F32)
    total = total + lax.dot_general(before, env, dims, preferred_element_type=F32)
    boundary_ref[0, 0] = total * (1.0 / size**0.5)
    third_ref[0, 0] = vector
    second_ref[0, 0] = combine(second, us)
    image_ref[0, 0] = combine(image, us)
    for place, value in enumerate(values):
        coef_ref[:, place : place + 1] = value


def kernel_call(body, out_shape, n_in, hbm=(), scratch=(), flops=0, moved=0):
    def spec(k):
        return pl.BlockSpec(memory_space=pl.ANY if k in hbm else pltpu.VMEM)

    return pl.pallas_call(
        body,
        out_shape=out_shape,
        in_specs=[spec(k) for k in range(n_in)],
        out_specs=jax.tree.map(lambda _: pl.BlockSpec(memory_space=pltpu.VMEM), out_shape),
        scratch_shapes=scratch,
        compiler_params=pltpu.CompilerParams(vmem_limit_bytes=24 << 20),
        cost_estimate=pl.CostEstimate(flops=flops, bytes_accessed=moved, transcendentals=0),
    )


def body(psi, sector_dims, env_left, env_right):
    size = psi.shape[-1]
    count, segs = lax.axis_size("sec"), lax.axis_size("seg")
    entries = float(count * size * size)

    def block(dtype, rows=size):
        return jax.ShapeDtypeStruct((rows, size), dtype)

    eight = jax.ShapeDtypeStruct((8, 128), F32)
    ways = routes(count)
    late = list(ways)[2:]
    last_ways = [ways[n] for n in late]
    onward = [(g, (g + 1) % segs) for g in range(segs)]
    product = 2 * 2 * size**3 * W_HOP

    def in_hbm(a):
        return pltpu.with_memory_space_constraint(a, pltpu.HBM)

    x, low, mask = kernel_call(
        start_kernel,
        (block(F32), block(BF16), block(F32)),
        2,
        hbm=(0, 1),
        scratch=[
            pltpu.VMEM((size, size), F32),
            pltpu.SMEM((1, 2), jnp.int32),
            pltpu.SemaphoreType.DMA((1 + PARTS,)),
        ],
        moved=2**20,
    )(in_hbm(psi), in_hbm(sector_dims))
    us = [x]
    for step in range(3):
        found = {}
        for n, way in ways.items():
            found[n] = permute(low, way)
        if step == 1:
            prev01 = lax.ppermute(pack, "seg", onward)
        if step == 2:
            dots = kernel_call(gram_kernel, eight, 3)(*us)
            prior = lax.ppermute(dots, "seg", onward)
            prev2 = lax.ppermute(low, "seg", onward)
        if step == 0:
            slots = 1 + len(ways)
            held = pltpu.VMEM((slots * W_HOP, size, size), BF16)
            total, left, right = kernel_call(
                functools.partial(load_kernel, [ways["across"], ways["first"]] + [ways[n] for n in late]),
                (block(F32), held, held),
                4,
                hbm=(0, 1),
                scratch=[pltpu.SemaphoreType.DMA((2 * slots,))],
                flops=2 * product,
                moved=8 << 20,
            )(in_hbm(env_left), in_hbm(env_right), low, found["across"])
        else:
            total = kernel_call(early_kernel, block(F32), 4, flops=2 * product)(
                left, right, low, found["across"]
            )
        total = kernel_call(middle_kernel, block(F32), 4, flops=product)(
            left, right, total, found["first"]
        )
        args = (left, right, mask, total, *[found[n] for n in late])
        n = len(late)
        if step == 0:
            u, low, pack = kernel_call(
                functools.partial(late_kernel, last_ways, True),
                (block(F32), block(BF16), block(BF16, 2 * size)),
                5 + n,
                flops=n * product,
            )(*args, low)
        elif step == 1:
            u, low = kernel_call(
                functools.partial(late_kernel, last_ways, False),
                (block(F32), block(BF16)),
                4 + n,
                flops=n * product,
            )(*args)
        else:
            u, top = kernel_call(
                functools.partial(last_kernel, last_ways),
                (block(F32), eight),
                7 + n,
                flops=n * product,
            )(*args, *us)
        us.append(u)
    sums = kernel_call(join_kernel, jax.ShapeDtypeStruct((24, 128), F32), 3)(dots, top, prior)
    hop = 1
    while hop < count:
        sums = sums + lax.ppermute(sums, "sec", [(i, i ^ hop) for i in range(count)])
        hop *= 2
    full = jax.ShapeDtypeStruct((1, 1, size, size), F32)
    return tuple(
        kernel_call(
            functools.partial(end_kernel, entries),
            (full, full, full, jax.ShapeDtypeStruct((1, 5), F32), full),
            8,
            flops=6 * size**3,
        )(sums, *us, left, prev01, prev2)
    )


def solution(mesh):
    count = mesh.shape["sec"]
    assert count & (count - 1) == 0
    in_specs = (
        P("seg", "sec", None, None),
        P("seg", "sec", None),
        P("seg", "sec", None, None, None),
        P("seg", "sec", None, None, None),
    )
    out_specs = (
        P("seg", "sec", None, None),
        P("seg", "sec", None, None),
        P("seg", "sec", None, None),
        P("seg", None),
        P("seg", "sec", None, None),
    )
    return jax.shard_map(body, mesh=mesh, in_specs=in_specs, out_specs=out_specs, check_vma=False)
```

```python
import functools

import jax
import jax.numpy as jnp
from jax import lax
from jax.experimental import pallas as pl
from jax.experimental.pallas import tpu as pltpu
from jax.sharding import PartitionSpec as P


W_ZERO = 6
W_HOP = 6
GRID = 4
EPSILON = 1e-06
PARTS = 2
SCALE = 2.0**-13
LOW_PAIRS = ((0, 0), (0, 1), (1, 1), (0, 2), (1, 2), (2, 2))
TOP_PAIRS = ((0, 3), (1, 3), (2, 3))

F32 = jnp.float32
BF16 = jnp.bfloat16


def routes(count):
    rows = count // GRID
    assert rows % 2 == 0 and GRID == 4
    first, across, second, between = {}, {}, {}, {}
    for s in range(count):
        r, c = divmod(s, GRID)
        over = s + GRID if r % 2 == 0 else s - GRID
        side = s + 1 if c == 1 else s - 1
        across[s] = s + 1 if c % 2 == 0 else s - 1
        if c in (0, GRID - 1):
            first[s] = over
        else:
            first[s], second[s] = side, over
        beyond = s - GRID if r % 2 == 0 else s + GRID
        if 0 <= beyond < count:
            between[s] = beyond
    found = {"first": first, "across": across, "second": second}
    if between:
        found["between"] = between
    return found


def permute(block, route):
    segs, count = lax.axis_size("seg"), lax.axis_size("sec")
    pairs = []
    for g in range(segs):
        for target in range(count):
            if target in route:
                pairs.append((g * count + route[target], g * count + target))
            else:
                pairs.append(((g ^ 1) * count + target, g * count + target))
    return lax.ppermute(block, ("seg", "sec"), pairs)


def reached(route):
    s = lax.axis_index("sec")
    return functools.reduce(jnp.logical_or, [s == t for t in route])


def first_term(route):
    place = {-1: 0, 1: 1, -GRID: 2, GRID: 3}
    s = lax.axis_index("sec")
    start = jnp.int32(0)
    for target, source in route.items():
        start = jnp.where(s == target, W_ZERO + W_HOP * place[source - target], start)
    return start


def split(value):
    high = value.astype(BF16)
    return high, (value - high.astype(F32)).astype(BF16)


def beside(parts):
    return jnp.concatenate(parts, axis=1)


def contract(left, right, block, rest=None, fine=False):
    n, size = left.shape[0], left.shape[1]
    tall = left.reshape(n * size, size)
    inner = jnp.dot(tall, block, preferred_element_type=F32)
    if rest is not None:
        inner = inner + jnp.dot(tall, rest, preferred_element_type=F32)
    pieces = split(inner) if fine else (inner.astype(BF16),)
    a = beside([p[w * size : (w + 1) * size] for p in pieces for w in range(n)])
    b = beside([right[w] for w in range(n)] * len(pieces))
    return lax.dot_general(a, b, (((1,), (1,)), ((), ())), preferred_element_type=F32)


def slot(ref, k):
    return ref[k * W_HOP : (k + 1) * W_HOP]


def row_dot(a, b):
    total = jnp.sum(a * b, axis=0, keepdims=True)
    return sum(total[:, k : k + 128] for k in range(0, total.shape[1], 128))


def start_kernel(psi_hbm, dims_hbm, x_ref, low_ref, mask_ref, psi_ref, dims_ref, sems):
    tall = psi_ref.shape[0] // PARTS
    copies = [pltpu.make_async_copy(dims_hbm.at[0], dims_ref, sems.at[0])]
    for k in range(PARTS):
        part = pl.ds(k * tall, tall)
        copies.append(
            pltpu.make_async_copy(psi_hbm.at[0, 0, part], psi_ref.at[part], sems.at[1 + k])
        )
    for c in copies:
        c.start()
    copies[0].wait()
    cols = lax.broadcasted_iota(jnp.int32, (tall, psi_ref.shape[1]), 1)
    live = cols < dims_ref[0, 1]
    for k in range(PARTS):
        part = pl.ds(k * tall, tall)
        rows = k * tall + lax.broadcasted_iota(jnp.int32, live.shape, 0)
        keep = live & (rows < dims_ref[0, 0])
        mask_ref[part] = jnp.where(keep, SCALE, 0.0)
        copies[1 + k].wait()
        x = jnp.where(keep, psi_ref[part], 0.0)
        x_ref[part] = x
        low_ref[part] = x.astype(BF16)


def load_kernel(
    ways, left_hbm, right_hbm, low_ref, across_ref, total_ref, left_ref, right_ref, sems
):
    starts = [0] + [first_term(w) for w in ways]
    copies = []
    for k, start in enumerate(starts):
        for side, (hbm, ref) in enumerate(((left_hbm, left_ref), (right_hbm, right_ref))):
            copies.append(
                pltpu.make_async_copy(
                    hbm.at[0, 0, pl.ds(start, W_HOP)],
                    ref.at[pl.ds(k * W_HOP, W_HOP)],
                    sems.at[2 * k + side],
                )
            )
    for c in copies:
        c.start()
    for c in copies[:2]:
        c.wait()
    total = contract(slot(left_ref, 0), slot(right_ref, 0), low_ref[...])
    for c in copies[2:4]:
        c.wait()
    total_ref[...] = total + contract(slot(left_ref, 1), slot(right_ref, 1), across_ref[...])
    for c in copies[4:]:
        c.wait()


def early_kernel(left_ref, right_ref, low_ref, across_ref, out_ref):
    out_ref[...] = contract(slot(left_ref, 0), slot(right_ref, 0), low_ref[...]) + contract(
        slot(left_ref, 1), slot(right_ref, 1), across_ref[...]
    )


def middle_kernel(left_ref, right_ref, total_ref, block_ref, out_ref):
    out_ref[...] = total_ref[...] + contract(
        slot(left_ref, 2), slot(right_ref, 2), block_ref[...]
    )


def image_into(u_ref, low_ref, after, ways, left_ref, right_ref, mask_ref, total_ref, blocks):
    def part(k):
        return contract(slot(left_ref, 3 + k), slot(right_ref, 3 + k), blocks[k][...])

    def finish(total):
        u = total * mask_ref[...]
        u_ref[...] = u
        if low_ref is not None:
            low_ref[...] = u.astype(BF16)
        if after is not None:
            after(u)

    so_far = total_ref
    for k, way in enumerate(ways[:-1]):
        if k == 0:
            u_ref[...] = total_ref[...]
            so_far = u_ref

        @pl.when(reached(way))
        def _():
            u_ref[...] += part(k)

    here = reached(ways[-1])

    @pl.when(here)
    def _():
        finish(so_far[...] + part(len(ways) - 1))

    @pl.when(jnp.logical_not(here))
    def _():
        finish(so_far[...])


def late_kernel(ways, packed, left_ref, right_ref, mask_ref, total_ref, *refs):
    n = len(ways)
    if packed:
        before_ref, u_ref, low_ref, pack_ref = refs[n:]
    else:
        u_ref, low_ref = refs[n:]
    image_into(u_ref, low_ref, None, ways, left_ref, right_ref, mask_ref, total_ref, refs[:n])
    if packed:
        size = low_ref.shape[0]
        pack_ref[:size] = before_ref[...]
        pack_ref[size:] = low_ref[...]


def last_kernel(ways, left_ref, right_ref, mask_ref, total_ref, *refs):
    n = len(ways)
    u0_ref, u1_ref, u2_ref, u_ref, dots_ref = refs[n:]
    dots_ref[...] = jnp.zeros_like(dots_ref)

    def after(u):
        for place, ref in enumerate((u0_ref, u1_ref, u2_ref)):
            dots_ref[place : place + 1] = row_dot(ref[...], u)

    image_into(u_ref, None, after, ways, left_ref, right_ref, mask_ref, total_ref, refs[:n])


def gram_kernel(u0_ref, u1_ref, u2_ref, dots_ref):
    u = [r[...] for r in (u0_ref, u1_ref, u2_ref)]
    dots_ref[...] = jnp.zeros_like(dots_ref)
    for place, (i, j) in enumerate(LOW_PAIRS):
        dots_ref[place : place + 1] = row_dot(u[i], u[j])


def join_kernel(low_ref, top_ref, prior_ref, out_ref):
    out_ref[:8] = low_ref[...]
    out_ref[8:16] = top_ref[...]
    out_ref[16:] = prior_ref[...]


def table_of(sums, low, top=None):
    table = {}
    for first, pairs in ((low, LOW_PAIRS), (top, TOP_PAIRS)):
        if first is not None:
            for place, (i, j) in enumerate(pairs):
                row = sums[first + place : first + place + 1]
                table[i, j] = table[j, i] = jnp.sum(row, axis=(0, 1), keepdims=True)
    return table


def apply(c):
    return [None] + [None if a is None else a * (1.0 / SCALE) for a in c]


def solve(table, entries):
    def dot(c, d):
        out = jnp.zeros((1, 1), F32)
        for i, a in enumerate(c):
            for j, b in enumerate(d):
                if a is not None and b is not None:
                    out = out + a * b * table[i, j]
        return out

    inv = 1.0 / entries
    v0 = [1.0 / jnp.sqrt(table[0, 0] * inv + EPSILON)]
    w = apply(v0)
    alpha0 = dot(w, v0) * inv
    r = [-alpha0 * v0[0], w[1]]
    beta0 = jnp.sqrt(dot(r, r) * inv + EPSILON)
    second = [c / beta0 for c in r]
    w = apply(second)
    alpha1 = dot(w, second) * inv
    r = [-alpha1 * second[0] - beta0 * v0[0], w[1] - alpha1 * second[1], w[2]]
    beta1 = jnp.sqrt(dot(r, r) * inv + EPSILON)
    third = [c / beta1 for c in r]
    values = [alpha0, alpha1, None, beta0, beta1]
    image = apply(third)
    if (0, 3) in table:
        values[2] = dot(image, third) * inv
    return second, third, image, values


def combine(coefs, blocks):
    out = None
    for c, b in zip(coefs, blocks):
        if c is not None:
            out = c * b if out is None else out + c * b
    return out


def end_kernel(
    entries, sums_ref, u0_ref, u1_ref, u2_ref, u3_ref, left_ref, prev01_ref, prev2_ref,
    second_ref, third_ref, image_ref, coef_ref, boundary_ref,
):
    sums = sums_ref[...]
    second, third, image, values = solve(table_of(sums, 0, 8), entries)
    _, prior, _, _ = solve(table_of(sums, 16), entries)
    us = [r[...] for r in (u0_ref, u1_ref, u2_ref, u3_ref)]
    size = us[0].shape[0]
    vector = combine(third, us)
    own = vector.astype(BF16)
    lows = (prev01_ref[:size], prev01_ref[size:], prev2_ref[...])
    before = combine(prior, [v.astype(F32) for v in lows])
    before = jnp.where(lax.axis_index("seg") > 0, before, 0.0).astype(BF16)
    env = jnp.dot(left_ref[0], own, preferred_element_type=F32).astype(BF16)
    dims = (((0,), (0,)), ((), ()))
    total = lax.dot_general(own, env, dims, preferred_element_type=F32)
    total = total + lax.dot_general(before, env, dims, preferred_element_type=F32)
    boundary_ref[0, 0] = total * (1.0 / size**0.5)
    third_ref[0, 0] = vector
    second_ref[0, 0] = combine(second, us)
    image_ref[0, 0] = combine(image, us)
    for place, value in enumerate(values):
        coef_ref[:, place : place + 1] = value


def kernel_call(body, out_shape, n_in, hbm=(), scratch=(), flops=0, moved=0):
    def spec(k):
        return pl.BlockSpec(memory_space=pl.ANY if k in hbm else pltpu.VMEM)

    return pl.pallas_call(
        body,
        out_shape=out_shape,
        in_specs=[spec(k) for k in range(n_in)],
        out_specs=jax.tree.map(lambda _: pl.BlockSpec(memory_space=pltpu.VMEM), out_shape),
        scratch_shapes=scratch,
        compiler_params=pltpu.CompilerParams(vmem_limit_bytes=24 << 20),
        cost_estimate=pl.CostEstimate(flops=flops, bytes_accessed=moved, transcendentals=0),
    )


def body(psi, sector_dims, env_left, env_right):
    size = psi.shape[-1]
    count, segs = lax.axis_size("sec"), lax.axis_size("seg")
    entries = float(count * size * size)

    def block(dtype, rows=size):
        return jax.ShapeDtypeStruct((rows, size), dtype)

    eight = jax.ShapeDtypeStruct((8, 128), F32)
    ways = routes(count)
    late = list(ways)[2:]
    last_ways = [ways[n] for n in late]
    onward = [(g, (g + 1) % segs) for g in range(segs)]
    product = 2 * 2 * size**3 * W_HOP

    def in_hbm(a):
        return pltpu.with_memory_space_constraint(a, pltpu.HBM)

    x, low, mask = kernel_call(
        start_kernel,
        (block(F32), block(BF16), block(F32)),
        2,
        hbm=(0, 1),
        scratch=[
            pltpu.VMEM((size, size), F32),
            pltpu.SMEM((1, 2), jnp.int32),
            pltpu.SemaphoreType.DMA((1 + PARTS,)),
        ],
        moved=2**20,
    )(in_hbm(psi), in_hbm(sector_dims))
    us = [x]
    for step in range(3):
        found = {}
        for n, way in ways.items():
            found[n] = permute(low, way)
        if step == 1:
            prev01 = lax.ppermute(pack, "seg", onward)
        if step == 2:
            dots = kernel_call(gram_kernel, eight, 3)(*us)
            prior = lax.ppermute(dots, "seg", onward)
            prev2 = lax.ppermute(low, "seg", onward)
        if step == 0:
            slots = 1 + len(ways)
            held = pltpu.VMEM((slots * W_HOP, size, size), BF16)
            total, left, right = kernel_call(
                functools.partial(load_kernel, [ways["across"], ways["first"]] + [ways[n] for n in late]),
                (block(F32), held, held),
                4,
                hbm=(0, 1),
                scratch=[pltpu.SemaphoreType.DMA((2 * slots,))],
                flops=2 * product,
                moved=8 << 20,
            )(in_hbm(env_left), in_hbm(env_right), low, found["across"])
        else:
            total = kernel_call(early_kernel, block(F32), 4, flops=2 * product)(
                left, right, low, found["across"]
            )
        total = kernel_call(middle_kernel, block(F32), 4, flops=product)(
            left, right, total, found["first"]
        )
        args = (left, right, mask, total, *[found[n] for n in late])
        n = len(late)
        if step == 0:
            u, low, pack = kernel_call(
                functools.partial(late_kernel, last_ways, True),
                (block(F32), block(BF16), block(BF16, 2 * size)),
                5 + n,
                flops=n * product,
            )(*args, low)
        elif step == 1:
            u, low = kernel_call(
                functools.partial(late_kernel, last_ways, False),
                (block(F32), block(BF16)),
                4 + n,
                flops=n * product,
            )(*args)
        else:
            u, top = kernel_call(
                functools.partial(last_kernel, last_ways),
                (block(F32), eight),
                7 + n,
                flops=n * product,
            )(*args, *us)
        us.append(u)
    sums = kernel_call(join_kernel, jax.ShapeDtypeStruct((24, 128), F32), 3)(dots, top, prior)
    hop = 1
    while hop < count:
        sums = sums + lax.ppermute(sums, "sec", [(i, i ^ hop) for i in range(count)])
        hop *= 2
    full = jax.ShapeDtypeStruct((1, 1, size, size), F32)
    return tuple(
        kernel_call(
            functools.partial(end_kernel, entries),
            (full, full, full, jax.ShapeDtypeStruct((1, 5), F32), full),
            8,
            flops=6 * size**3,
        )(sums, *us, left, prev01, prev2)
    )


def solution(mesh):
    count = mesh.shape["sec"]
    assert count & (count - 1) == 0
    in_specs = (
        P("seg", "sec", None, None),
        P("seg", "sec", None),
        P("seg", "sec", None, None, None),
        P("seg", "sec", None, None, None),
    )
    out_specs = (
        P("seg", "sec", None, None),
        P("seg", "sec", None, None),
        P("seg", "sec", None, None),
        P("seg", None),
        P("seg", "sec", None, None),
    )
    return jax.shard_map(body, mesh=mesh, in_specs=in_specs, out_specs=out_specs, check_vma=False)
```
